128 devices in a mesh: seq: 8 (over z, core), head: 16 (over y, x).
Axes of the slice: x: 4, y: 4, z: 4, core: 2. Of those that a mesh axis runs over, the one named last changes fastest.
Arguments:
- query: bfloat16 [65536, 2048], P('seq', 'head'), may hold values from -4.5 to 4.5
- keys: bfloat16 [65536, 2048], P('seq', 'head'), may hold values from -4.5 to 4.5
- values: bfloat16 [65536, 2048], P('seq', 'head'), may hold values from -6 to 6
- mem_init: float32 [16, 128, 128], P('head'), may hold values from -362.03867 to 362.03867
- beta: float32 [16], P('head'), may hold values from -2 to 2
- mem_gain: float32 [2048], P('head'), may hold values from 0.1 to 1.9
- loc_gain: float32 [2048], P('head'), may hold values from 0.1 to 1.9
- w_out: bfloat16 [2048, 2048], P('head'), may hold values from -0.125 to 0.125
Outputs:
- attn_out: bfloat16 [65536, 2048], P(('seq', 'head'))
- memory_prefix: float32 [8, 16, 128, 128], P('seq', 'head')
The draws below stay inside these ranges and needn't reach their ends.
All inputs are finite; a program needn't handle non-finite values.
Results may differ from the reference program's by a relative error of at most 0.0054.
Values may be sent and summed in bfloat16 or wider, within the bound.
A program may use at most 128 MiB of HBM per device.

```python
import jax
import jax.numpy as jnp
from jax import lax

H = 16
HD = 128
SEG = 2048
SEGS_DEV = 4
D = 2048
TOK_DEV = 8192
TOKENS = 65536


def drawn_pair(key):
    query_key = jax.random.fold_in(key, 11)
    keys_key = jax.random.fold_in(key, 12)
    query = jnp.clip(jax.random.normal(query_key, (TOKENS, D), jnp.float32), -4.5, 4.5)
    keys = jnp.clip(jax.random.normal(keys_key, (TOKENS, D), jnp.float32), -4.5, 4.5)
    return (query, keys)


def draw_query(key, part):
    return drawn_pair(key)[0].astype(jnp.bfloat16)


def draw_keys(key, part):
    return drawn_pair(key)[1].astype(jnp.bfloat16)


def steps_of(key, extent, cuts, smallest, high):
    factor_of, own = 1.0, jax.random.fold_in(key, 6)
    for position, parts in cuts:
        draws = jnp.exp(jax.random.uniform(jax.random.fold_in(own, position), (parts,), jnp.float32, smallest / len(cuts), high / len(cuts)))
        factor_of = factor_of * jnp.repeat(draws, extent[position] // parts).reshape([-1 if axis == position else 1 for axis in range(len(extent))])
    return factor_of


def noise(key, dims, deviation, most, cuts=(), kind=jnp.bfloat16):
    entries = jax.random.normal(key, dims, jnp.float32) * deviation
    if len(cuts) > 0:
        entries = steps_of(key, dims, cuts, -0.22, 0.18) * entries
    return jnp.clip(entries, min=-most, max=most).astype(kind)


def setup_inputs(seed: int = 0) -> dict:
    key_of = jax.random.split(jax.random.key(seed), 9)
    return {
        "query": draw_query(jax.random.fold_in(key_of[8], 71), 0),
        "keys": draw_keys(jax.random.fold_in(key_of[8], 71), 0),
        "values": noise(key_of[2], (TOKENS, D), 1.0, 6.0, ((0, 8), (1, 16))),
        "mem_init": noise(key_of[3], (H, HD, HD), (TOK_DEV ** 0.5), 362.03867, ((0, 16),), jnp.float32),
        "beta": jnp.clip(jax.random.uniform(key_of[4], (H,), jnp.float32, -2.0, 2.0) * steps_of(key_of[4], (H,), ((0, 16),), -0.4, 0.0), -2.0, 2.0),
        "mem_gain": jnp.clip(1.0 + 0.18 * jax.random.normal(key_of[5], (D,), jnp.float32), 0.1, 1.9),
        "loc_gain": jnp.clip(1.0 + 0.18 * jax.random.normal(key_of[6], (D,), jnp.float32), 0.1, 1.9),
        "w_out": noise(key_of[7], (D, D), D ** -0.5, 0.125, ((0, 16),)),
    }


def elu_feature(source):
    return (jax.nn.elu(source.astype(jnp.float32)) + 1.0).astype(jnp.bfloat16)

def rms_norm(source, gain_vec):
    mean_sq = lax.optimization_barrier(jnp.mean(source * source, axis=-1, keepdims=True))
    return source * lax.rsqrt(mean_sq + 1e-06) * gain_vec

def segment_attention(q_seg, k_seg, v_seg):
    length = q_seg.shape[0]
    scores = jnp.dot(q_seg, k_seg.T, preferred_element_type=jnp.float32) * HD ** (-0.5)
    row_pos = lax.broadcasted_iota(jnp.int32, (length, length), 0)
    col_pos = lax.broadcasted_iota(jnp.int32, (length, length), 1)
    scores = jnp.where(col_pos <= row_pos, scores, -jnp.inf)
    largest = lax.optimization_barrier(jnp.max(scores, axis=-1, keepdims=True))
    weights = jnp.exp(scores - largest)
    denominator = lax.optimization_barrier(jnp.sum(weights, axis=-1, keepdims=True))
    probabilities = (weights / denominator).astype(jnp.bfloat16)
    return jnp.dot(probabilities, v_seg, preferred_element_type=jnp.float32)

def reference(query, keys, values, mem_init, beta, mem_gain, loc_gain, w_out):
    seg_total = TOKENS // SEG

    def one_head(head_pos):

        def column(source):
            return lax.dynamic_slice_in_dim(source, head_pos * HD, HD, 1).reshape(seg_total, SEG, HD)
        q_head = column(query)
        k_head = column(keys)
        v_head = column(values)

        def attend(triple):
            return segment_attention(triple[0], triple[1], triple[2])
        local = lax.map(attend, (q_head, k_head, v_head))
        q_feat = elu_feature(q_head).astype(jnp.float32)
        k_feat = elu_feature(k_head).astype(jnp.float32)
        kv_terms = jnp.einsum('nsa,nsb->nab', k_feat, v_head.astype(jnp.float32), precision=lax.Precision.HIGHEST)
        inclusive = jnp.cumsum(kv_terms, axis=0)
        earlier = jnp.concatenate([jnp.zeros((1, HD, HD), jnp.float32), inclusive[:-1]], axis=0)
        memory = mem_init[head_pos] + earlier
        read = jnp.einsum('nsa,nab->nsb', q_feat, memory, precision=lax.Precision.HIGHEST)
        gate_value = jax.nn.sigmoid(beta[head_pos])
        m_gain = lax.dynamic_slice_in_dim(mem_gain, head_pos * HD, HD)
        l_gain = lax.dynamic_slice_in_dim(loc_gain, head_pos * HD, HD)
        mixed = gate_value * rms_norm(read, m_gain) + (1.0 - gate_value) * rms_norm(local, l_gain)
        head_out = mixed.astype(jnp.bfloat16).reshape(TOKENS, HD)
        prefix = memory[::SEGS_DEV] * TOK_DEV ** (-0.5)
        return (head_out, prefix)
    head_outs, prefixes = lax.map(one_head, jnp.arange(H, dtype=jnp.int32))
    joined = jnp.transpose(head_outs, (1, 0, 2)).reshape(TOKENS, H * HD)
    attn_out = jnp.dot(joined, w_out, preferred_element_type=jnp.float32).astype(jnp.bfloat16)
    return (attn_out, jnp.transpose(prefixes, (1, 0, 2, 3)))
```

```python
import functools
import math

import jax
import jax.numpy as jnp
from jax import lax
from jax.experimental import pallas as pl
from jax.experimental.pallas import tpu as pltpu
from jax.sharding import PartitionSpec as P

HD = 128
SEG = 2048
BLK = 512
D = 2048
NSEG = 4
NX = 4
EPS = 1e-06
MESH = pl.DeviceIdType.MESH
F32 = jnp.float32
BF16 = jnp.bfloat16
C2 = HD**-0.5 * math.log2(math.e)


def gray(t):
    return t + (t // 2) * (1 - 2 * lax.rem(t, 2))


def attend(b, base, q_ref, k_ref, v_ref, s_ref, acc_ref):
    half = BLK // 2
    q = q_ref[pl.ds(pl.multiple_of(base + b * BLK, BLK), BLK), :]

    def score(row0, rows, key0, cols, masked):
        k = k_ref[pl.ds(pl.multiple_of(base + key0, 256), cols), :]
        s = lax.dot_general(
            q[row0 : row0 + rows], k, (((1,), (1,)), ((), ())), preferred_element_type=F32
        )
        s = s * C2
        if masked:
            col = lax.broadcasted_iota(jnp.int32, (rows, cols), 1) + (key0 - b * BLK)
            row = lax.broadcasted_iota(jnp.int32, (rows, cols), 0) + row0
            s = jnp.where(col <= row, s, -jnp.inf)
        s_ref[row0 : row0 + rows, key0 : key0 + cols] = s
        top = s[:, 0:128]
        for t in range(1, cols // 128):
            top = jnp.maximum(top, s[:, t * 128 : (t + 1) * 128])
        return top

    tops = [None, None]

    def merge(i, top):
        tops[i] = top if tops[i] is None else jnp.maximum(tops[i], top)

    for key0 in range(0, b * BLK, BLK):
        top = score(0, BLK, key0, BLK, False)
        merge(0, top[:half])
        merge(1, top[half:])
    merge(1, score(half, half, b * BLK, half, False))
    merge(0, score(0, half, b * BLK, half, True))
    merge(1, score(half, half, b * BLK + half, half, True))
    for i in range(2):
        largest = jnp.max(tops[i], axis=1, keepdims=True)
        length = b * BLK + (i + 1) * half
        rows = slice(i * half, (i + 1) * half)
        p = jnp.exp2(s_ref[rows, 0:length] - largest).astype(BF16)
        v = v_ref[pl.ds(pl.multiple_of(base, SEG), length), :]
        v = jnp.concatenate([v, jnp.ones((length, HD), BF16)], axis=1)
        acc_ref[rows, :] = jnp.dot(p, v, preferred_element_type=F32)


def feature(x):
    x = x.astype(F32)
    return jnp.where(x > 0, x + 1.0, jnp.exp(x)).astype(BF16)


def kernel(
    beta_ref, q_hbm, k_hbm, v_hbm, init_ref, mg_ref, lg_ref, w_hbm,
    out_hbm, prefix_ref,
    q_ref, k_ref, v_ref, kv_ref, tot_ref, trecv, base_ref, memcat, s_ref, acc_ref,
    ho, recv, w4, oacc, o_ref,
    lsem, wsem, osem,
    a_s, a_r, b_s, b_r, z_s, z_r, c_s, c_r, t_s, t_r, h_s, h_r,
):
    s = lax.axis_index("seq")
    h = lax.axis_index("head")
    z, c = s // 2, lax.rem(s, 2)
    y, x = h // NX, lax.rem(h, NX)
    par = lax.rem(z, 2)

    def at(v, d):
        return lax.rem(v + d, NX)

    def head_dev(dy, dx):
        return (s, at(y, dy) * NX + at(x, dx))

    def z_dev(d):
        return (at(z, d) * 2 + c, h)

    mate = (z * 2 + (1 - c), h)

    def remote(src, dst, ssem, rsem, dev):
        return pltpu.make_async_remote_copy(
            src_ref=src, dst_ref=dst, send_sem=ssem, recv_sem=rsem,
            device_id=dev, device_id_type=MESH,
        )

    def rows_of(p, half):
        return pl.ds(pl.multiple_of((2 * p + c) * 32 + 16 * half, 16), 16)

    barrier = pltpu.get_barrier_semaphore()

    def greet_head(i, carry):
        pl.semaphore_signal(
            barrier, inc=1, device_id=(s, lax.rem(h + i, 16)), device_id_type=MESH
        )
        return carry

    lax.fori_loop(1, 16, greet_head, 0)

    def greet_seq(i, carry):
        pl.semaphore_signal(
            barrier, inc=1, device_id=(lax.rem(s + i, 8), h), device_id_type=MESH
        )
        return carry

    lax.fori_loop(1, 8, greet_seq, 0)

    def load(which, n):
        src = (k_hbm, v_hbm, q_hbm)[which]
        dst = (k_ref, v_ref, q_ref)[which]
        span = pl.ds(n * SEG, SEG)
        return pltpu.make_async_copy(src.at[span], dst.at[span], lsem.at[which * NSEG + n])

    for n in range(NSEG):
        load(0, n).start()
        load(1, n).start()
    own = [
        pltpu.make_async_copy(
            w_hbm.at[rows_of(par, half)], w4.at[y, x, rows_of(par, half), :], wsem.at[half]
        )
        for half in range(2)
    ]
    for copy in own:
        copy.start()
    for n in range(NSEG):
        load(2, n).start()

    def stage_a(i):
        half, d = i // 3, i % 3 + 1
        dev = head_dev(0, d) if half == 0 else head_dev(d, 0)
        return remote(
            w_hbm.at[rows_of(par, half)], w4.at[y, x, rows_of(par, half), :],
            a_s.at[i], a_r.at[i], dev,
        )

    def chunk(half, place, p):
        if half == 0:
            return w4.at[place, :, rows_of(p, 0), :]
        return w4.at[:, place, rows_of(p, 1), :]

    def stage_b(i):
        half, d = i // 3, i % 3 + 1
        ref = chunk(half, y if half == 0 else x, par)
        dev = head_dev(d, 0) if half == 0 else head_dev(0, d)
        return remote(ref, ref, b_s.at[i], b_r.at[i], dev)

    def place_of(half, d):
        return at(y if half == 0 else x, NX - d)

    def stage_z(half, d):
        ref = chunk(half, place_of(half, d), par)
        return remote(
            ref, ref, z_s.at[half * 4 + d], z_r.at[half * 4 + d], z_dev(1 if half == 0 else 3)
        )

    def stage_c(kind, half, d):
        ref = chunk(half, place_of(half, d), par if kind == 0 else 1 - par)
        i = kind * 8 + half * 4 + d
        return remote(ref, ref, c_s.at[i], c_r.at[i], mate)

    def prefix_send(d):
        return remote(
            tot_ref, trecv.at[d - 1], t_s.at[d - 1], t_r.at[d - 1], (lax.rem(s + d, 8), h)
        )

    def kv_term(n):
        load(0, n).wait()
        load(1, n).wait()
        span = slice(n * SEG, (n + 1) * SEG)
        kv_ref[n] = lax.dot_general(
            feature(k_ref[span, :]), v_ref[span, :], (((0,), (0,)), ((), ())),
            preferred_element_type=F32,
        )

    kv_term(0)
    pl.semaphore_wait(barrier, 22)
    for i in (0, 2, 3, 5, 1, 4):
        stage_a(i).start()
    for n in range(1, NSEG):
        kv_term(n)
    tot_ref[...] = (kv_ref[0] + kv_ref[1]) + (kv_ref[2] + kv_ref[3])
    for d in range(1, 8):

        @pl.when(s + d < 8)
        def _(d=d):
            prefix_send(d).start()

    for copy in own:
        copy.wait()
    for i in range(6):
        stage_a(i).wait_recv()
    for i in (0, 3, 2, 5, 1, 4):
        stage_b(i).start()
    for half in range(2):
        stage_z(half, 0).start()
        stage_c(0, half, 0).start()
    for n in range(NSEG):
        load(2, n).wait()

    gate = 1.0 / (1.0 + jnp.exp(-jnp.full((1, HD), beta_ref[0], F32)))
    mem_scale = gate * mg_ref[...]
    loc_scale = (1.0 - gate) * lg_ref[...]

    def step(k, carry):
        dy, dx = gray(3 - k // NX), gray(3 - lax.rem(k, NX))
        n, b = at(y, dy), at(x, dx)
        base = pl.multiple_of(n * SEG, SEG)
        for bb in range(4):

            @pl.when(b == bb)
            def _(bb=bb):
                attend(bb, base, q_ref, k_ref, v_ref, s_ref, acc_ref)

        @pl.when(k == 0)
        def _():
            base_ref[...] = init_ref[0]
            for d in range(1, 8):

                @pl.when(s - d >= 0)
                def _(d=d):
                    prefix_send(d).wait_recv()
                    base_ref[...] += trecv[d - 1]

            running = base_ref[...]
            prefix_ref[0, 0] = running * (NSEG * SEG) ** -0.5
            for m in range(NSEG):
                top = running.astype(BF16)
                memcat[m, 0:HD, :] = top
                memcat[m, HD : 2 * HD, :] = (running - top.astype(F32)).astype(BF16)
                if m < NSEG - 1:
                    running = running + kv_ref[m]

        feat = feature(q_ref[pl.ds(pl.multiple_of(base + b * BLK, BLK), BLK), :])
        read = jnp.dot(
            jnp.concatenate([feat, feat], axis=1), memcat[n], preferred_element_type=F32
        )
        read_sq = jnp.mean(read * read, axis=-1, keepdims=True)
        total = acc_ref[:, 0:HD]
        weight = acc_ref[:, HD : HD + 1]
        total_sq = jnp.mean(total * total, axis=-1, keepdims=True)
        mixed = (read * lax.rsqrt(read_sq + EPS)) * mem_scale + (
            total * lax.rsqrt(total_sq + EPS * (weight * weight))
        ) * loc_scale
        mixed = mixed.astype(BF16)

        @pl.when(k < 15)
        def _():
            ho[k] = mixed
            send_block(k).start()

        @pl.when(k == 15)
        def _():
            recv[15] = mixed

        @pl.when(k == 5)
        def _():
            for half in range(2):
                for d in (1, 3):
                    stage_b(half * 3 + d - 1).wait_recv()
                    stage_z(half, d).start()
                    stage_c(0, half, d).start()
                stage_z(half, 0).wait_recv()
                stage_c(1, half, 0).start()

        @pl.when(k == 10)
        def _():
            for half in range(2):
                stage_b(half * 3 + 1).wait_recv()
                stage_z(half, 2).start()
                stage_c(0, half, 2).start()

        @pl.when(k == 14)
        def _():
            for half in range(2):
                for d in (1, 3):
                    stage_z(half, d).wait_recv()
                    stage_c(1, half, d).start()

        return carry

    def send_block(k):
        dy, dx = gray(3 - k // NX), gray(3 - lax.rem(k, NX))
        return remote(ho.at[k], recv.at[k], h_s.at[k], h_r.at[k], head_dev(dy, dx))

    lax.fori_loop(0, 16, step, 0)
    for half in range(2):
        stage_z(half, 2).wait_recv()
        stage_c(1, half, 2).start()
    for kind in range(2):
        for half in range(2):
            for d in range(4):
                stage_c(kind, half, d).wait_recv()

    def project(g, first, last):
        for i in range(4):
            if 4 * g + i < 15:
                send_block(4 * g + i).wait_recv()
        dy = gray(3 - g)
        yy = at(y, NX - dy)
        xs = [at(x, NX - int(e)) for e in (2, 3, 1, 0)]
        act = jnp.concatenate([recv[4 * g + i] for i in range(4)], axis=1)
        for j in range(4):
            cols = slice(j * 512, (j + 1) * 512)
            wt = jnp.concatenate([w4[yy, xx, :, cols] for xx in xs], axis=0)
            r = jnp.dot(act, wt, preferred_element_type=F32)
            if not first:
                r = oacc[:, cols] + r
            if last:
                o_ref[:, cols] = r.astype(BF16)
                put(j).start()
            else:
                oacc[:, cols] = r

    def put(j):
        cols = pl.ds(j * 512, 512)
        return pltpu.make_async_copy(o_ref.at[:, cols], out_hbm.at[:, cols], osem.at[j])

    for g in range(4):
        project(g, g == 0, g == 3)

    for i in range(6):
        stage_a(i).wait_send()
        stage_b(i).wait_send()
    for half in range(2):
        for d in range(4):
            stage_z(half, d).wait_send()
            stage_c(0, half, d).wait_send()
            stage_c(1, half, d).wait_send()
    for d in range(1, 8):

        @pl.when(s + d < 8)
        def _(d=d):
            prefix_send(d).wait_send()

    def sent(k, carry):
        send_block(k).wait_send()
        return carry

    lax.fori_loop(0, 15, sent, 0)
    for j in range(4):
        put(j).wait()


def per_device(query, keys, values, mem_init, beta, mem_gain, loc_gain, w_out):
    tokens = query.shape[0]
    any_spec = pl.BlockSpec(memory_space=pl.ANY)
    vmem = pl.BlockSpec(memory_space=pltpu.VMEM)
    dma = pltpu.SemaphoreType.DMA
    attn_out, prefix = pl.pallas_call(
        kernel,
        out_shape=(
            jax.ShapeDtypeStruct((BLK, D), BF16),
            jax.ShapeDtypeStruct((1, 1, HD, HD), F32),
        ),
        in_specs=[
            pl.BlockSpec(memory_space=pltpu.SMEM),
            any_spec, any_spec, any_spec, vmem, vmem, vmem, any_spec,
        ],
        out_specs=(any_spec, vmem),
        scratch_shapes=[
            pltpu.VMEM((tokens, HD), BF16),
            pltpu.VMEM((tokens, HD), BF16),
            pltpu.VMEM((tokens, HD), BF16),
            pltpu.VMEM((NSEG, HD, HD), F32),
            pltpu.VMEM((HD, HD), F32),
            pltpu.VMEM((7, HD, HD), F32),
            pltpu.VMEM((HD, HD), F32),
            pltpu.VMEM((NSEG, 2 * HD, HD), BF16),
            pltpu.VMEM((BLK, SEG), F32),
            pltpu.VMEM((BLK, 2 * HD), F32),
            pltpu.VMEM((15, BLK, HD), BF16),
            pltpu.VMEM((16, BLK, HD), BF16),
            pltpu.VMEM((NX, NX, HD, D), BF16),
            pltpu.VMEM((BLK, D), F32),
            pltpu.VMEM((BLK, D), BF16),
            dma((12,)), dma((2,)), dma((4,)),
            dma((6,)), dma((6,)), dma((6,)), dma((6,)), dma((8,)), dma((8,)),
            dma((16,)), dma((16,)), dma((7,)), dma((7,)), dma((15,)), dma((15,)),
        ],
        compiler_params=pltpu.CompilerParams(
            collective_id=0, has_side_effects=True, vmem_limit_bytes=60 * 2**20
        ),
        name="layer",
    )(
        beta, query, keys, values, mem_init,
        mem_gain.reshape(1, HD), loc_gain.reshape(1, HD), w_out,
    )
    return attn_out, prefix


def solution(mesh):
    in_specs = (
        P("seq", "head"),
        P("seq", "head"),
        P("seq", "head"),
        P("head", None, None),
        P("head"),
        P("head"),
        P("head"),
        P("head", None),
    )
    out_specs = (P(("seq", "head"), None), P("seq", "head", None, None))
    return jax.shard_map(
        per_device, mesh=mesh, in_specs=in_specs, out_specs=out_specs, check_vma=False
    )
```

```python
import functools
import math

import jax
import jax.numpy as jnp
from jax import lax
from jax.experimental import pallas as pl
from jax.experimental.pallas import tpu as pltpu
from jax.sharding import PartitionSpec as P

HD = 128
SEG = 2048
BLK = 512
D = 2048
NSEG = 4
NX = 4
WS = 256
EPS = 1e-06
MESH = pl.DeviceIdType.MESH
F32 = jnp.float32
BF16 = jnp.bfloat16
C2 = HD**-0.5 * math.log2(math.e)


def attend(b, base, q_ref, k_ref, v_ref, s_ref, acc_ref):
    half = BLK // 2
    q = q_ref[pl.ds(pl.multiple_of(base + b * BLK, BLK), BLK), :]

    def score(row0, rows, key0, cols, masked):
        k = k_ref[pl.ds(pl.multiple_of(base + key0, 256), cols), :]
        s = lax.dot_general(
            q[row0 : row0 + rows], k, (((1,), (1,)), ((), ())), preferred_element_type=F32
        )
        s = s * C2
        if masked:
            col = lax.broadcasted_iota(jnp.int32, (rows, cols), 1) + (key0 - b * BLK)
            row = lax.broadcasted_iota(jnp.int32, (rows, cols), 0) + row0
            s = jnp.where(col <= row, s, -jnp.inf)
        s_ref[row0 : row0 + rows, key0 : key0 + cols] = s
        top = s[:, 0:128]
        for t in range(1, cols // 128):
            top = jnp.maximum(top, s[:, t * 128 : (t + 1) * 128])
        return top

    tops = [None, None]

    def merge(i, top):
        tops[i] = top if tops[i] is None else jnp.maximum(tops[i], top)

    for key0 in range(0, b * BLK, BLK):
        top = score(0, BLK, key0, BLK, False)
        merge(0, top[:half])
        merge(1, top[half:])
    merge(1, score(half, half, b * BLK, half, False))
    merge(0, score(0, half, b * BLK, half, True))
    merge(1, score(half, half, b * BLK + half, half, True))
    for i in range(2):
        largest = jnp.max(tops[i], axis=1, keepdims=True)
        length = b * BLK + (i + 1) * half
        rows = slice(i * half, (i + 1) * half)
        p = jnp.exp2(s_ref[rows, 0:length] - largest).astype(BF16)
        v = v_ref[pl.ds(pl.multiple_of(base, SEG), length), :]
        v = jnp.concatenate([v, jnp.ones((length, HD), BF16)], axis=1)
        acc_ref[rows, :] = jnp.dot(p, v, preferred_element_type=F32)


def feature(x):
    x = x.astype(F32)
    return jnp.where(x > 0, x + 1.0, jnp.exp(x)).astype(BF16)


ORDER = (
    (2, 2), (1, 1), (3, 3), (3, 1), (1, 3), (1, 2), (2, 1), (3, 2),
    (2, 3), (1, 0), (3, 0), (2, 0), (0, 1), (0, 3), (0, 2), (0, 0),
)
HOLD = 4
SERVICE = {
    1: (("own", 3),),
    3: (("own", 4),),
    4: (("own", 5), ("z", 0), ("z", 1), ("z", 2)),
    7: (("z", 3),),
    11: (("z", 4),),
    14: (("z", 5),),
}


def pick(k, table):
    if isinstance(k, int):
        return table[k]
    value = jnp.int32(table[0])
    for i in range(1, len(table)):
        value = jnp.where(k == i, jnp.int32(table[i]), value)
    return value


def kernel(
    beta_ref, q_hbm, k_hbm, v_hbm, init_hbm, mg_hbm, lg_hbm, w_hbm,
    out_ref, prefix_ref,
    q_ref, k_ref, v_ref, kv_ref, tot_ref, trecv, base_ref, memcat, s_ref, acc_ref,
    ho, recv, w8, oacc,
    init_ref, mg_ref, lg_ref, lsem, wsem, psem,
    a_s, a_r, z_s, z_r, r_s, r_r, c_s, c_r, t_s, t_r, h_s, h_r,
):
    s = lax.axis_index("seq")
    h = lax.axis_index("head")
    z, c = s // 2, lax.rem(s, 2)
    y, x = h // NX, lax.rem(h, NX)

    def at(v, d):
        return lax.rem(v + d, NX)

    def head_dev(dy, dx):
        return (s, at(y, dy) * NX + at(x, dx))

    def z_dev(d):
        return (at(z, d) * 2 + c, h)

    mate = (z * 2 + (1 - c), h)

    def remote(src, dst, ssem, rsem, dev):
        return pltpu.make_async_remote_copy(
            src_ref=src, dst_ref=dst, send_sem=ssem, recv_sem=rsem,
            device_id=dev, device_id_type=MESH,
        )

    barrier = pltpu.get_barrier_semaphore()

    def greet_head(i, carry):
        pl.semaphore_signal(
            barrier, inc=1, device_id=(s, lax.rem(h + i, 16)), device_id_type=MESH
        )
        return carry

    lax.fori_loop(1, 16, greet_head, 0)

    def greet_seq(i, carry):
        pl.semaphore_signal(
            barrier, inc=1, device_id=(lax.rem(s + i, 8), h), device_id_type=MESH
        )
        return carry

    lax.fori_loop(1, 8, greet_seq, 0)

    def load(which, n):
        src = (k_hbm, v_hbm, q_hbm)[which]
        dst = (k_ref, v_ref, q_ref)[which]
        span = pl.ds(n * SEG, SEG)
        return pltpu.make_async_copy(src.at[span], dst.at[span], lsem.at[which * NSEG + n])

    def slice_of(dz):
        return at(z, dz) * 2 + c

    def own(i):
        sl = lax.rem(slice_of(0) + i, 8)
        return pltpu.make_async_copy(
            w_hbm.at[:, pl.ds(pl.multiple_of(sl * WS, WS), WS)], w8.at[sl, y, x], wsem.at[i]
        )

    own(0).start()
    for n in range(NSEG):
        load(0, n).start()
        load(1, n).start()

    def stage_a(dy, dx):
        ref = w8.at[slice_of(0), y, x]
        i = dy * NX + dx
        return remote(ref, ref, a_s.at[i], a_r.at[i], head_dev(dy, dx))

    PIECES = ((0, 1), (0, 3), (0, 2), (1, None), (3, None), (2, None))

    def piece(dz, p):
        dy, dx = PIECES[p]
        if dx is None:
            return w8.at[slice_of(dz), at(y, NX - dy)]
        return w8.at[slice_of(dz), y, at(x, NX - dx)]

    def stage_z(p, way):
        ref = piece(0, p)
        return remote(
            ref, ref, z_s.at[p * 2 + way], z_r.at[p * 2 + way], z_dev(1 if way == 0 else 3)
        )

    def upward(p):
        return PIECES[p][0] in (0, 3)

    def stage_r(p):
        ref = piece(3 if upward(p) else 1, p)
        return remote(ref, ref, r_s.at[p], r_r.at[p], z_dev(1 if upward(p) else 3))

    def stage_c(dz, p):
        ref = piece(dz, p)
        return remote(ref, ref, c_s.at[dz * 6 + p], c_r.at[dz * 6 + p], mate)

    def forward_own(p):
        dy, dx = PIECES[p]
        for d in range(NX) if dx is None else (dx,):
            stage_a(dy, d).wait_recv()
        stage_z(p, 0).start()
        stage_z(p, 1).start()
        stage_c(0, p).start()

    def forward_z(p):
        stage_z(p, 0).wait_recv()
        if upward(p):
            stage_r(p).start()
        stage_c(3, p).start()
        stage_z(p, 1).wait_recv()
        if not upward(p):
            stage_r(p).start()
        stage_c(1, p).start()

    def forward_r(p):
        stage_r(p).wait_recv()
        stage_c(2, p).start()

    def prefix_send(d):
        return remote(
            tot_ref, trecv.at[d - 1], t_s.at[d - 1], t_r.at[d - 1], (lax.rem(s + d, 8), h)
        )

    def kv_term(n):
        load(0, n).wait()
        load(1, n).wait()
        span = slice(n * SEG, (n + 1) * SEG)
        kv_ref[n] = lax.dot_general(
            feature(k_ref[span, :]), v_ref[span, :], (((0,), (0,)), ((), ())),
            preferred_element_type=F32,
        )

    own(0).wait()
    pl.semaphore_wait(barrier, 22)
    for dy in (0, 1, 3, 2):
        for dx in (1, 3, 0, 2):
            if dy or dx:
                stage_a(dy, dx).start()
    for n in range(NSEG):
        load(2, n).start()
    for i in range(1, 8):
        own(i).start()
    small = [
        pltpu.make_async_copy(src, dst, psem.at[i])
        for i, (src, dst) in enumerate(
            ((init_hbm, init_ref), (mg_hbm, mg_ref), (lg_hbm, lg_ref))
        )
    ]
    for copy in small:
        copy.start()
    for n in range(NSEG):
        kv_term(n)
    tot_ref[...] = (kv_ref[0] + kv_ref[1]) + (kv_ref[2] + kv_ref[3])
    for d in range(1, 8):

        @pl.when(s + d < 8)
        def _(d=d):
            prefix_send(d).start()

    for n in range(NSEG):
        load(2, n).wait()
    for copy in small:
        copy.wait()
    for i in range(1, 8):
        own(i).wait()
    for p in range(3):
        forward_own(p)

    gate = 1.0 / (1.0 + jnp.exp(-jnp.full((1, HD), beta_ref[0], F32)))
    mem_scale = gate * mg_ref[...]
    loc_scale = (1.0 - gate) * lg_ref[...]

    def offsets(k):
        return pick(k, [o[0] for o in ORDER]), pick(k, [o[1] for o in ORDER])

    def send_block(k):
        dy, dx = offsets(k)
        return remote(ho.at[k], recv.at[k], h_s.at[k], h_r.at[k], head_dev(dy, dx))

    def step(k, carry):
        dy, dx = offsets(k)
        n, b = at(y, dy), at(x, dx)
        base = pl.multiple_of(n * SEG, SEG)
        for bb in range(4):

            @pl.when(b == bb)
            def _(bb=bb):
                attend(bb, base, q_ref, k_ref, v_ref, s_ref, acc_ref)

        @pl.when(k == 0)
        def _():
            base_ref[...] = init_ref[0]
            for d in range(1, 8):

                @pl.when(s - d >= 0)
                def _(d=d):
                    prefix_send(d).wait_recv()
                    base_ref[...] += trecv[d - 1]

            running = base_ref[...]
            prefix_ref[0, 0] = running * (NSEG * SEG) ** -0.5
            for m in range(NSEG):
                top = running.astype(BF16)
                memcat[m, 0:HD, :] = top
                memcat[m, HD : 2 * HD, :] = (running - top.astype(F32)).astype(BF16)
                if m < NSEG - 1:
                    running = running + kv_ref[m]

        feat = feature(q_ref[pl.ds(pl.multiple_of(base + b * BLK, BLK), BLK), :])
        read = jnp.dot(
            jnp.concatenate([feat, feat], axis=1), memcat[n], preferred_element_type=F32
        )
        read_sq = jnp.mean(read * read, axis=-1, keepdims=True)
        total = acc_ref[:, 0:HD]
        weight = acc_ref[:, HD : HD + 1]
        total_sq = jnp.mean(total * total, axis=-1, keepdims=True)
        mixed = (read * lax.rsqrt(read_sq + EPS)) * mem_scale + (
            total * lax.rsqrt(total_sq + EPS * (weight * weight))
        ) * loc_scale
        mixed = mixed.astype(BF16)

        @pl.when(k < 15)
        def _():
            ho[k] = mixed

        @pl.when(k == 15)
        def _():
            recv[15] = mixed

        for when, todo in SERVICE.items():

            @pl.when(k == when)
            def _(todo=todo):
                for what, p in todo:
                    (forward_own if what == "own" else forward_z)(p)

        @pl.when(k == HOLD)
        def _():
            def send(i, carry):
                send_block(i).start()
                return carry

            lax.fori_loop(0, HOLD, send, 0)

        @pl.when((k >= HOLD) & (k < 15))
        def _():
            send_block(k).start()

        return carry

    lax.fori_loop(0, 16, step, 0)

    def slice_at(j):
        dz = pick(j // 2, [0, 3, 1, 2])
        return at(z, dz) * 2 + lax.rem(c + j, 2)

    def arrived(g):
        for i in range(4 * g, min(4 * g + 4, 15)):
            send_block(i).wait_recv()

    def project(slots, js, first, last):
        act = jnp.concatenate([recv[i] for i in slots], axis=1)
        for j in js:
            sl = slice_at(j)
            cols = pl.ds(pl.multiple_of(sl * WS, WS), WS)
            wt = [w8[sl, at(y, NX - ORDER[i][0]), at(x, NX - ORDER[i][1])] for i in slots]
            r = jnp.dot(act, jnp.concatenate(wt, axis=0), preferred_element_type=F32)
            if not first:
                r = oacc[:, cols] + r
            if last:
                out_ref[:, cols] = r.astype(BF16)
            else:
                oacc[:, cols] = r

    near, far = range(6), range(6, 8)
    early = [i for i in range(16) if ORDER[i][0] in (0, 1)]
    late = [i for i in range(16) if ORDER[i][0] in (3, 2)]
    for dz in (0, 3, 1):
        for p in range(6):
            stage_c(dz, p).wait_recv()
    arrived(0)
    project(range(0, 4), near, True, False)
    arrived(1)
    project(range(4, 8), near, False, False)
    for p in (0, 1, 2, 3):
        forward_r(p)
    arrived(2)
    project(range(8, 12), near, False, False)
    for p in (4, 5):
        forward_r(p)
    arrived(3)
    project(range(12, 16), near, False, True)
    for p in (0, 1, 2, 3):
        stage_c(2, p).wait_recv()
    project(early, far, True, False)
    for p in (4, 5):
        stage_c(2, p).wait_recv()
    project(late, far, False, True)

    for dy in range(NX):
        for dx in range(NX):
            if dy or dx:
                stage_a(dy, dx).wait_send()
    for p in range(6):
        stage_z(p, 0).wait_send()
        stage_z(p, 1).wait_send()
        stage_r(p).wait_send()
        for dz in range(4):
            stage_c(dz, p).wait_send()
    for d in range(1, 8):

        @pl.when(s + d < 8)
        def _(d=d):
            prefix_send(d).wait_send()

    def sent(k, carry):
        send_block(k).wait_send()
        return carry

    lax.fori_loop(0, 15, sent, 0)


def per_device(query, keys, values, mem_init, beta, mem_gain, loc_gain, w_out):
    tokens = query.shape[0]
    hbm = pl.BlockSpec(memory_space=pltpu.HBM)
    vmem = pl.BlockSpec(memory_space=pltpu.VMEM)
    dma = pltpu.SemaphoreType.DMA
    attn_out, prefix = pl.pallas_call(
        kernel,
        out_shape=(
            pltpu.VMEM((BLK, D), BF16),
            pltpu.VMEM((1, 1, HD, HD), F32),
        ),
        in_specs=[
            pl.BlockSpec(memory_space=pltpu.SMEM),
            hbm, hbm, hbm, hbm, hbm, hbm, hbm,
        ],
        out_specs=(vmem, vmem),
        scratch_shapes=[
            pltpu.VMEM((tokens, HD), BF16),
            pltpu.VMEM((tokens, HD), BF16),
            pltpu.VMEM((tokens, HD), BF16),
            pltpu.VMEM((NSEG, HD, HD), F32),
            pltpu.VMEM((HD, HD), F32),
            pltpu.VMEM((7, HD, HD), F32),
            pltpu.VMEM((HD, HD), F32),
            pltpu.VMEM((NSEG, 2 * HD, HD), BF16),
            pltpu.VMEM((BLK, SEG), F32),
            pltpu.VMEM((BLK, 2 * HD), F32),
            pltpu.VMEM((15, BLK, HD), BF16),
            pltpu.VMEM((16, BLK, HD), BF16),
            pltpu.VMEM((8, NX, NX, HD, WS), BF16),
            pltpu.VMEM((BLK, D), F32),
            pltpu.VMEM((1, HD, HD), F32),
            pltpu.VMEM((1, HD), F32),
            pltpu.VMEM((1, HD), F32),
            dma((12,)), dma((8,)), dma((3,)),
            dma((16,)), dma((16,)), dma((12,)), dma((12,)), dma((6,)), dma((6,)),
            dma((24,)), dma((24,)), dma((7,)), dma((7,)), dma((15,)), dma((15,)),
        ],
        compiler_params=pltpu.CompilerParams(
            collective_id=0, has_side_effects=True, vmem_limit_bytes=52 * 2**20
        ),
        name="layer",
    )(
        beta, query, keys, values, mem_init,
        mem_gain.reshape(1, HD), loc_gain.reshape(1, HD), w_out,
    )
    return attn_out, prefix


def solution(mesh):
    in_specs = (
        P("seq", "head"),
        P("seq", "head"),
        P("seq", "head"),
        P("head", None, None),
        P("head"),
        P("head"),
        P("head"),
        P("head", None),
    )
    out_specs = (P(("seq", "head"), None), P("seq", "head", None, None))
    return jax.shard_map(
        per_device, mesh=mesh, in_specs=in_specs, out_specs=out_specs, check_vma=False
    )
```

```python
import functools
import math

import jax
import jax.numpy as jnp
from jax import lax
from jax.experimental import pallas as pl
from jax.experimental.pallas import tpu as pltpu
from jax.sharding import PartitionSpec as P

HD = 128
SEG = 2048
BLK = 512
D = 2048
NSEG = 4
NX = 4
WS = 256
EPS = 1e-06
MESH = pl.DeviceIdType.MESH
F32 = jnp.float32
BF16 = jnp.bfloat16
C2 = HD**-0.5 * math.log2(math.e)


def attend(b, base, q_ref, k_ref, v_ref, s_ref, acc_ref):
    half = BLK // 2
    q = q_ref[pl.ds(pl.multiple_of(base + b * BLK, BLK), BLK), :]

    def score(row0, rows, key0, cols, masked):
        k = k_ref[pl.ds(pl.multiple_of(base + key0, 256), cols), :]
        s = lax.dot_general(
            q[row0 : row0 + rows], k, (((1,), (1,)), ((), ())), preferred_element_type=F32
        )
        s = s * C2
        if masked:
            col = lax.broadcasted_iota(jnp.int32, (rows, cols), 1) + (key0 - b * BLK)
            row = lax.broadcasted_iota(jnp.int32, (rows, cols), 0) + row0
            s = jnp.where(col <= row, s, -jnp.inf)
        s_ref[row0 : row0 + rows, key0 : key0 + cols] = s
        top = s[:, 0:128]
        for t in range(1, cols // 128):
            top = jnp.maximum(top, s[:, t * 128 : (t + 1) * 128])
        return top

    tops = [None, None]

    def merge(i, top):
        tops[i] = top if tops[i] is None else jnp.maximum(tops[i], top)

    for key0 in range(0, b * BLK, BLK):
        top = score(0, BLK, key0, BLK, False)
        merge(0, top[:half])
        merge(1, top[half:])
    merge(1, score(half, half, b * BLK, half, False))
    merge(0, score(0, half, b * BLK, half, True))
    merge(1, score(half, half, b * BLK + half, half, True))
    for i in range(2):
        largest = jnp.max(tops[i], axis=1, keepdims=True)
        length = b * BLK + (i + 1) * half
        rows = slice(i * half, (i + 1) * half)
        p = jnp.exp2(s_ref[rows, 0:length] - largest).astype(BF16)
        v = v_ref[pl.ds(pl.multiple_of(base, SEG), length), :]
        v = jnp.concatenate([v, jnp.ones((length, HD), BF16)], axis=1)
        acc_ref[rows, :] = jnp.dot(p, v, preferred_element_type=F32)


def feature(x):
    x = x.astype(F32)
    return jnp.where(x > 0, x + 1.0, jnp.exp(x)).astype(BF16)


ORDER = (
    (2, 2), (1, 1), (3, 3), (3, 1), (1, 3), (1, 2), (2, 1), (3, 2),
    (2, 3), (1, 0), (3, 0), (2, 0), (0, 1), (0, 3), (0, 2), (0, 0),
)
HOLD = 4
SERVICE = {
    1: (("own", 3),),
    3: (("own", 4),),
    4: (("own", 5), ("z", 0), ("z", 1), ("z", 2)),
    7: (("z", 3),),
    11: (("z", 4),),
    14: (("z", 5),),
}


def pick(k, table):
    if isinstance(k, int):
        return table[k]
    value = jnp.int32(table[0])
    for i in range(1, len(table)):
        value = jnp.where(k == i, jnp.int32(table[i]), value)
    return value


def kernel(
    beta_ref, q_hbm, k_hbm, v_hbm, init_hbm, mg_hbm, lg_hbm, w_hbm,
    out_ref, prefix_ref,
    q_ref, k_ref, v_ref, kv_ref, tot_ref, chip_ref, trecv, base_ref, memcat, s_ref, acc_ref,
    ho, recv, w8, oacc,
    init_ref, mg_ref, lg_ref, lsem, wsem, psem,
    a_s, a_r, z_s, z_r, r_s, r_r, c_s, c_r, t_s, t_r, h_s, h_r,
):
    s = lax.axis_index("seq")
    h = lax.axis_index("head")
    z, c = s // 2, lax.rem(s, 2)
    y, x = h // NX, lax.rem(h, NX)

    def at(v, d):
        return lax.rem(v + d, NX)

    def head_dev(dy, dx):
        return (s, at(y, dy) * NX + at(x, dx))

    def z_dev(d):
        return (at(z, d) * 2 + c, h)

    mate = (z * 2 + (1 - c), h)

    def remote(src, dst, ssem, rsem, dev):
        return pltpu.make_async_remote_copy(
            src_ref=src, dst_ref=dst, send_sem=ssem, recv_sem=rsem,
            device_id=dev, device_id_type=MESH,
        )

    barrier = pltpu.get_barrier_semaphore()

    def greet_head(i, carry):
        pl.semaphore_signal(
            barrier, inc=1, device_id=(s, lax.rem(h + i, 16)), device_id_type=MESH
        )
        return carry

    lax.fori_loop(1, 16, greet_head, 0)

    for dev in (mate, z_dev(1), z_dev(2), z_dev(3)):
        pl.semaphore_signal(barrier, inc=1, device_id=dev, device_id_type=MESH)

    def load(which, n):
        src = (k_hbm, v_hbm, q_hbm)[which]
        dst = (k_ref, v_ref, q_ref)[which]
        span = pl.ds(n * SEG, SEG)
        return pltpu.make_async_copy(src.at[span], dst.at[span], lsem.at[which * NSEG + n])

    def slice_of(dz):
        return at(z, dz) * 2 + c

    def own(i):
        sl = lax.rem(slice_of(0) + i, 8)
        return pltpu.make_async_copy(
            w_hbm.at[:, pl.ds(pl.multiple_of(sl * WS, WS), WS)], w8.at[sl, y, x], wsem.at[i]
        )

    for n in range(NSEG):
        load(0, n).start()
        load(1, n).start()

    def stage_a(dy, dx):
        i = dy * NX + dx
        src = w_hbm.at[:, pl.ds(pl.multiple_of(slice_of(0) * WS, WS), WS)]
        return remote(
            src, w8.at[slice_of(0), y, x], a_s.at[i], a_r.at[i], head_dev(dy, dx)
        )

    PIECES = ((0, 1), (0, 3), (0, 2), (1, None), (3, None), (2, None))

    def piece(dz, p):
        dy, dx = PIECES[p]
        if dx is None:
            return w8.at[slice_of(dz), at(y, NX - dy)]
        return w8.at[slice_of(dz), y, at(x, NX - dx)]

    def stage_z(p, way):
        ref = piece(0, p)
        return remote(
            ref, ref, z_s.at[p * 2 + way], z_r.at[p * 2 + way], z_dev(1 if way == 0 else 3)
        )

    def upward(p):
        return PIECES[p][0] in (0, 3)

    def stage_r(p):
        ref = piece(3 if upward(p) else 1, p)
        return remote(ref, ref, r_s.at[p], r_r.at[p], z_dev(1 if upward(p) else 3))

    def stage_c(dz, p):
        ref = piece(dz, p)
        return remote(ref, ref, c_s.at[dz * 6 + p], c_r.at[dz * 6 + p], mate)

    def forward_own(p):
        dy, dx = PIECES[p]
        for d in range(NX) if dx is None else (dx,):
            stage_a(dy, d).wait_recv()
        stage_z(p, 0).start()
        stage_z(p, 1).start()
        stage_c(0, p).start()

    def forward_z(p):
        stage_z(p, 0).wait_recv()
        if upward(p):
            stage_r(p).start()
        stage_c(3, p).start()
        stage_z(p, 1).wait_recv()
        if not upward(p):
            stage_r(p).start()
        stage_c(1, p).start()

    def forward_r(p):
        stage_r(p).wait_recv()
        stage_c(2, p).start()

    def mate_send():
        return remote(tot_ref, trecv.at[0], t_s.at[0], t_r.at[0], mate)

    def prefix_send(d):
        return remote(chip_ref, trecv.at[d], t_s.at[d], t_r.at[d], z_dev(d))

    def kv_term(n):
        load(0, n).wait()
        load(1, n).wait()
        span = slice(n * SEG, (n + 1) * SEG)
        kv_ref[n] = lax.dot_general(
            feature(k_ref[span, :]), v_ref[span, :], (((0,), (0,)), ((), ())),
            preferred_element_type=F32,
        )

    pl.semaphore_wait(barrier, 19)
    for dy in (0, 1, 3, 2):
        for dx in (1, 3, 0, 2):
            if dy or dx:
                stage_a(dy, dx).start()
    for n in range(NSEG):
        load(2, n).start()
    for i in range(8):
        own(i).start()
    small = [
        pltpu.make_async_copy(src, dst, psem.at[i])
        for i, (src, dst) in enumerate(
            ((init_hbm, init_ref), (mg_hbm, mg_ref), (lg_hbm, lg_ref))
        )
    ]
    for copy in small:
        copy.start()
    for n in range(NSEG):
        kv_term(n)
    tot_ref[...] = (kv_ref[0] + kv_ref[1]) + (kv_ref[2] + kv_ref[3])
    mate_send().start()
    mate_send().wait_recv()
    chip_ref[...] = tot_ref[...] + trecv[0]
    for d in range(1, NX):

        @pl.when(z + d < NX)
        def _(d=d):
            prefix_send(d).start()

    for p in range(3):
        forward_own(p)
    for n in range(NSEG):
        load(2, n).wait()
    for copy in small:
        copy.wait()
    for i in range(8):
        own(i).wait()

    gate = 1.0 / (1.0 + jnp.exp(-jnp.full((1, HD), beta_ref[0], F32)))
    mem_scale = gate * mg_ref[...]
    loc_scale = (1.0 - gate) * lg_ref[...]

    def offsets(k):
        return pick(k, [o[0] for o in ORDER]), pick(k, [o[1] for o in ORDER])

    def send_block(k):
        dy, dx = offsets(k)
        return remote(ho.at[k], recv.at[k], h_s.at[k], h_r.at[k], head_dev(dy, dx))

    def step(k, carry):
        dy, dx = offsets(k)
        n, b = at(y, dy), at(x, dx)
        base = pl.multiple_of(n * SEG, SEG)
        for bb in range(4):

            @pl.when(b == bb)
            def _(bb=bb):
                attend(bb, base, q_ref, k_ref, v_ref, s_ref, acc_ref)

        @pl.when(k == 0)
        def _():
            base_ref[...] = init_ref[0]
            for d in range(1, NX):

                @pl.when(z - d >= 0)
                def _(d=d):
                    prefix_send(d).wait_recv()
                    base_ref[...] += trecv[d]

            @pl.when(c == 1)
            def _():
                base_ref[...] += trecv[0]

            running = base_ref[...]
            prefix_ref[0, 0] = running * (NSEG * SEG) ** -0.5
            for m in range(NSEG):
                top = running.astype(BF16)
                memcat[m, 0:HD, :] = top
                memcat[m, HD : 2 * HD, :] = (running - top.astype(F32)).astype(BF16)
                if m < NSEG - 1:
                    running = running + kv_ref[m]

        feat = feature(q_ref[pl.ds(pl.multiple_of(base + b * BLK, BLK), BLK), :])
        read = jnp.dot(
            jnp.concatenate([feat, feat], axis=1), memcat[n], preferred_element_type=F32
        )
        read_sq = jnp.mean(read * read, axis=-1, keepdims=True)
        total = acc_ref[:, 0:HD]
        weight = acc_ref[:, HD : HD + 1]
        total_sq = jnp.mean(total * total, axis=-1, keepdims=True)
        mixed = (read * lax.rsqrt(read_sq + EPS)) * mem_scale + (
            total * lax.rsqrt(total_sq + EPS * (weight * weight))
        ) * loc_scale
        mixed = mixed.astype(BF16)

        @pl.when(k < 15)
        def _():
            ho[k] = mixed

        @pl.when(k == 15)
        def _():
            recv[15] = mixed

        for when, todo in SERVICE.items():

            @pl.when(k == when)
            def _(todo=todo):
                for what, p in todo:
                    (forward_own if what == "own" else forward_z)(p)

        @pl.when(k == HOLD)
        def _():
            def send(i, carry):
                send_block(i).start()
                return carry

            lax.fori_loop(0, HOLD, send, 0)

        @pl.when((k >= HOLD) & (k < 15))
        def _():
            send_block(k).start()

        return carry

    lax.fori_loop(0, 16, step, 0)

    def slice_at(j):
        dz = pick(j // 2, [0, 3, 1, 2])
        return at(z, dz) * 2 + lax.rem(c + j, 2)

    def arrived(g):
        for i in range(4 * g, min(4 * g + 4, 15)):
            send_block(i).wait_recv()

    def project(slots, js, first, last):
        act = jnp.concatenate([recv[i] for i in slots], axis=1)
        for j in js:
            sl = slice_at(j)
            cols = pl.ds(pl.multiple_of(sl * WS, WS), WS)
            wt = [w8[sl, at(y, NX - ORDER[i][0]), at(x, NX - ORDER[i][1])] for i in slots]
            r = jnp.dot(act, jnp.concatenate(wt, axis=0), preferred_element_type=F32)
            if not first:
                r = oacc[:, cols] + r
            if last:
                out_ref[:, cols] = r.astype(BF16)
            else:
                oacc[:, cols] = r

    near, far = range(6), range(6, 8)
    done = [0, 1, 2, 3, 4, 5, 6, 7, 12, 13, 14, 15]
    early = [i for i in done if ORDER[i][0] in (0, 1)]
    late = [i for i in done if ORDER[i][0] in (3, 2)]
    for dz in (0, 3, 1):
        for p in range(6):
            stage_c(dz, p).wait_recv()
    arrived(0)
    project(range(0, 4), near, True, False)
    arrived(1)
    project(range(4, 8), near, False, False)
    for p in (0, 1, 2, 3):
        forward_r(p)
    arrived(3)
    project(range(12, 16), near, False, False)
    for p in (4, 5):
        forward_r(p)
    for p in (0, 1, 2, 3):
        stage_c(2, p).wait_recv()
    project(early, far, True, False)
    for p in (4, 5):
        stage_c(2, p).wait_recv()
    project(late, far, False, False)
    arrived(2)
    project(range(8, 12), range(8), False, True)

    for dy in range(NX):
        for dx in range(NX):
            if dy or dx:
                stage_a(dy, dx).wait_send()
    for p in range(6):
        stage_z(p, 0).wait_send()
        stage_z(p, 1).wait_send()
        stage_r(p).wait_send()
        for dz in range(4):
            stage_c(dz, p).wait_send()
    mate_send().wait_send()
    for d in range(1, NX):

        @pl.when(z + d < NX)
        def _(d=d):
            prefix_send(d).wait_send()

    def sent(k, carry):
        send_block(k).wait_send()
        return carry

    lax.fori_loop(0, 15, sent, 0)


def finish(a_ref, p_ref, a_out, p_out, sem):
    copies = [pltpu.make_async_copy(p_ref, p_out, sem.at[4])]
    for i in range(4):
        rows = pl.ds(i * 128, 128)
        copies.append(pltpu.make_async_copy(a_ref.at[rows], a_out.at[rows], sem.at[i]))
    for copy in copies:
        copy.start()
    for copy in copies:
        copy.wait()


def per_device(query, keys, values, mem_init, beta, mem_gain, loc_gain, w_out):
    tokens = query.shape[0]
    hbm = pl.BlockSpec(memory_space=pltpu.HBM)
    vmem = pl.BlockSpec(memory_space=pltpu.VMEM)
    dma = pltpu.SemaphoreType.DMA
    attn_out, prefix = pl.pallas_call(
        kernel,
        out_shape=(
            pltpu.VMEM((BLK, D), BF16),
            pltpu.VMEM((1, 1, HD, HD), F32),
        ),
        in_specs=[
            pl.BlockSpec(memory_space=pltpu.SMEM),
            hbm, hbm, hbm, hbm, hbm, hbm, hbm,
        ],
        out_specs=(vmem, vmem),
        scratch_shapes=[
            pltpu.VMEM((tokens, HD), BF16),
            pltpu.VMEM((tokens, HD), BF16),
            pltpu.VMEM((tokens, HD), BF16),
            pltpu.VMEM((NSEG, HD, HD), F32),
            pltpu.VMEM((HD, HD), F32),
            pltpu.VMEM((HD, HD), F32),
            pltpu.VMEM((NX, HD, HD), F32),
            pltpu.VMEM((HD, HD), F32),
            pltpu.VMEM((NSEG, 2 * HD, HD), BF16),
            pltpu.VMEM((BLK, SEG), F32),
            pltpu.VMEM((BLK, 2 * HD), F32),
            pltpu.VMEM((15, BLK, HD), BF16),
            pltpu.VMEM((16, BLK, HD), BF16),
            pltpu.VMEM((8, NX, NX, HD, WS), BF16),
            pltpu.VMEM((BLK, D), F32),
            pltpu.VMEM((1, HD, HD), F32),
            pltpu.VMEM((1, HD), F32),
            pltpu.VMEM((1, HD), F32),
            dma((12,)), dma((8,)), dma((3,)),
            dma((16,)), dma((16,)), dma((12,)), dma((12,)), dma((6,)), dma((6,)),
            dma((24,)), dma((24,)), dma((4,)), dma((4,)), dma((15,)), dma((15,)),
        ],
        compiler_params=pltpu.CompilerParams(
            collective_id=0, has_side_effects=True, vmem_limit_bytes=52 * 2**20
        ),
        name="layer",
    )(
        beta, query, keys, values, mem_init,
        mem_gain.reshape(1, HD), loc_gain.reshape(1, HD), w_out,
    )
    return pl.pallas_call(
        finish,
        out_shape=(
            jax.ShapeDtypeStruct((BLK, D), BF16),
            jax.ShapeDtypeStruct((1, 1, HD, HD), F32),
        ),
        in_specs=[vmem, vmem],
        out_specs=(hbm, hbm),
        scratch_shapes=[dma((5,))],
        name="finish",
    )(
        pltpu.with_memory_space_constraint(attn_out, pltpu.VMEM),
        pltpu.with_memory_space_constraint(prefix, pltpu.VMEM),
    )


def solution(mesh):
    in_specs = (
        P("seq", "head"),
        P("seq", "head"),
        P("seq", "head"),
        P("head", None, None),
        P("head"),
        P("head"),
        P("head"),
        P("head", None),
    )
    out_specs = (P(("seq", "head"), None), P("seq", "head", None, None))
    return jax.shard_map(
        per_device, mesh=mesh, in_specs=in_specs, out_specs=out_specs, check_vma=False
    )
```

```python
import functools
import math

import jax
import jax.numpy as jnp
from jax import lax
from jax.experimental import pallas as pl
from jax.experimental.pallas import tpu as pltpu
from jax.sharding import PartitionSpec as P

HD = 128
SEG = 2048
BLK = 512
D = 2048
NSEG = 4
NX = 4
WS = 256
EPS = 1e-06
MESH = pl.DeviceIdType.MESH
F32 = jnp.float32
BF16 = jnp.bfloat16
C2 = HD**-0.5 * math.log2(math.e)


def attend(b, base, q_ref, k_ref, v_ref, s_ref, acc_ref):
    half = BLK // 2
    q = q_ref[pl.ds(pl.multiple_of(base + b * BLK, BLK), BLK), :]

    def score(row0, rows, key0, cols, masked):
        k = k_ref[pl.ds(pl.multiple_of(base + key0, 256), cols), :]
        s = lax.dot_general(
            q[row0 : row0 + rows], k, (((1,), (1,)), ((), ())), preferred_element_type=F32
        )
        s = s * C2
        if masked:
            col = lax.broadcasted_iota(jnp.int32, (rows, cols), 1) + (key0 - b * BLK)
            row = lax.broadcasted_iota(jnp.int32, (rows, cols), 0) + row0
            s = jnp.where(col <= row, s, -jnp.inf)
        s_ref[row0 : row0 + rows, key0 : key0 + cols] = s
        top = s[:, 0:128]
        for t in range(1, cols // 128):
            top = jnp.maximum(top, s[:, t * 128 : (t + 1) * 128])
        return top

    tops = [None, None]

    def merge(i, top):
        tops[i] = top if tops[i] is None else jnp.maximum(tops[i], top)

    for key0 in range(0, b * BLK, BLK):
        top = score(0, BLK, key0, BLK, False)
        merge(0, top[:half])
        merge(1, top[half:])
    merge(1, score(half, half, b * BLK, half, False))
    merge(0, score(0, half, b * BLK, half, True))
    merge(1, score(half, half, b * BLK + half, half, True))
    for i in range(2):
        largest = jnp.max(tops[i], axis=1, keepdims=True)
        length = b * BLK + (i + 1) * half
        rows = slice(i * half, (i + 1) * half)
        p = jnp.exp2(s_ref[rows, 0:length] - largest).astype(BF16)
        v = v_ref[pl.ds(pl.multiple_of(base, SEG), length), :]
        v = jnp.concatenate([v, jnp.ones((length, HD), BF16)], axis=1)
        acc_ref[rows, :] = jnp.dot(p, v, preferred_element_type=F32)


def feature(x):
    x = x.astype(F32)
    return jnp.where(x > 0, x + 1.0, jnp.exp(x)).astype(BF16)


ORDER = (
    (2, 2), (1, 1), (3, 3), (3, 1), (1, 3), (1, 2), (2, 1), (3, 2),
    (2, 3), (1, 0), (3, 0), (2, 0), (0, 1), (0, 3), (0, 2), (0, 0),
)
HOLD = 3
LAST = (8, 9, 10, 11)
NEAR = ((0, 1), (0, 3), (1, 0), (3, 0))
NEAR_PIECE = (0, 1, 3, 4)
RELAY = (
    (2, 0, 2, True),
    (3, 1, 1, False), (3, 1, 3, False), (3, 1, 2, False),
    (4, 3, 1, True), (4, 3, 3, True), (4, 3, 2, True),
    (5, 2, 0, True), (5, 2, 1, True), (5, 2, 2, False), (5, 2, 3, False),
)
SERVICE = {
    1: (("own", 4),),
    3: (("own", 5), ("z", 0), ("z", 1), ("z", 2)),
    6: (("z", 3),),
    10: (("z", 4),),
    13: (("z", 5),),
}


def pick(k, table):
    if isinstance(k, int):
        return table[k]
    value = jnp.int32(table[0])
    for i in range(1, len(table)):
        value = jnp.where(k == i, jnp.int32(table[i]), value)
    return value


def kernel(
    beta_hbm, q_hbm, k_hbm, v_hbm, init_hbm, mg_hbm, lg_hbm, w_hbm,
    oacc, recv, w8, prefix_ref,
    q_ref, k_ref, v_ref, kv_ref, tot_ref, chip_ref, trecv, base_ref, memcat, s_ref, acc_ref,
    ho, beta_ref, init_ref, mg_ref, lg_ref, lsem, wsem, psem,
    a_s, a_r, z_s, z_r, r_s, r_r, e_s, e_r, c_s, c_r, t_s, t_r, h_s, h_r,
):
    s = lax.axis_index("seq")
    h = lax.axis_index("head")
    z, c = s // 2, lax.rem(s, 2)
    y, x = h // NX, lax.rem(h, NX)

    def at(v, d):
        return lax.rem(v + d, NX)

    def head_dev(dy, dx):
        return (s, at(y, dy) * NX + at(x, dx))

    def z_dev(d):
        return (at(z, d) * 2 + c, h)

    mate = (z * 2 + (1 - c), h)

    def remote(src, dst, ssem, rsem, dev):
        return pltpu.make_async_remote_copy(
            src_ref=src, dst_ref=dst, send_sem=ssem, recv_sem=rsem,
            device_id=dev, device_id_type=MESH,
        )

    barrier = pltpu.get_barrier_semaphore()

    def greet_head(i, carry):
        pl.semaphore_signal(
            barrier, inc=1, device_id=(s, lax.rem(h + i, 16)), device_id_type=MESH
        )
        return carry

    lax.fori_loop(1, 16, greet_head, 0)

    for dev in (mate, z_dev(1), z_dev(2), z_dev(3)):
        pl.semaphore_signal(barrier, inc=1, device_id=dev, device_id_type=MESH)

    def load(which, n):
        src = (k_hbm, v_hbm, q_hbm)[which]
        dst = (k_ref, v_ref, q_ref)[which]
        span = pl.ds(n * SEG, SEG)
        return pltpu.make_async_copy(src.at[span], dst.at[span], lsem.at[which * NSEG + n])

    def slice_of(dz):
        return at(z, dz) * 2 + c

    def own(i):
        sl = lax.rem(slice_of(0) + i, 8)
        return pltpu.make_async_copy(
            w_hbm.at[:, pl.ds(pl.multiple_of(sl * WS, WS), WS)], w8.at[sl, y, x], wsem.at[i]
        )

    for n in range(NSEG):
        load(0, n).start()
        load(1, n).start()

    def stage_a(dy, dx):
        i = dy * NX + dx
        src = w_hbm.at[:, pl.ds(pl.multiple_of(slice_of(0) * WS, WS), WS)]
        return remote(
            src, w8.at[slice_of(0), y, x], a_s.at[i], a_r.at[i], head_dev(dy, dx)
        )

    PIECES = ((0, 1), (0, 3), (0, 2), (1, None), (3, None), (2, None))

    def piece(dz, p):
        dy, dx = PIECES[p]
        if dx is None:
            return w8.at[slice_of(dz), at(y, NX - dy)]
        return w8.at[slice_of(dz), y, at(x, NX - dx)]

    def stage_z(p, way):
        ref = piece(0, p)
        return remote(
            ref, ref, z_s.at[p * 2 + way], z_r.at[p * 2 + way], z_dev(1 if way == 0 else 3)
        )

    def stage_e(i):
        dy, dx = NEAR[i]
        sl = slice_of(2)
        src = w_hbm.at[:, pl.ds(pl.multiple_of(sl * WS, WS), WS)]
        return remote(src, w8.at[sl, y, x], e_s.at[i], e_r.at[i], head_dev(dy, dx))

    def stage_r(i):
        _, dy, dx, up = RELAY[i]
        ref = w8.at[slice_of(3 if up else 1), at(y, NX - dy), at(x, NX - dx)]
        return remote(ref, ref, r_s.at[i], r_r.at[i], z_dev(1 if up else 3))

    def stage_c(dz, p):
        ref = piece(dz, p)
        return remote(ref, ref, c_s.at[dz * 6 + p], c_r.at[dz * 6 + p], mate)

    def forward_own(p):
        dy, dx = PIECES[p]
        for d in range(NX) if dx is None else (dx,):
            stage_a(dy, d).wait_recv()
        stage_z(p, 0).start()
        stage_z(p, 1).start()
        stage_c(0, p).start()

    def forward_z(p):
        for way in range(2):
            stage_z(p, way).wait_recv()
            for i, (piece_of, _, _, up) in enumerate(RELAY):
                if piece_of == p and up == (way == 0):
                    stage_r(i).start()
            stage_c(3 if way == 0 else 1, p).start()

    def forward_r(p):
        if p in NEAR_PIECE:
            stage_e(NEAR_PIECE.index(p)).wait_recv()
        for i, relay in enumerate(RELAY):
            if relay[0] == p:
                stage_r(i).wait_recv()
        stage_c(2, p).start()

    def mate_send():
        return remote(tot_ref, trecv.at[0], t_s.at[0], t_r.at[0], mate)

    def prefix_send(d):
        return remote(chip_ref, trecv.at[d], t_s.at[d], t_r.at[d], z_dev(d))

    def kv_term(n):
        load(0, n).wait()
        load(1, n).wait()
        span = slice(n * SEG, (n + 1) * SEG)
        kv_ref[n] = lax.dot_general(
            feature(k_ref[span, :]), v_ref[span, :], (((0,), (0,)), ((), ())),
            preferred_element_type=F32,
        )

    pl.semaphore_wait(barrier, 19)
    for dy in (0, 1, 3, 2):
        for dx in (1, 3, 0, 2):
            if dy or dx:
                stage_a(dy, dx).start()
    for i in range(4):
        stage_e(i).start()
    for n in range(NSEG):
        load(2, n).start()
    for i in range(8):
        own(i).start()
    small = [
        pltpu.make_async_copy(src, dst, psem.at[i])
        for i, (src, dst) in enumerate(
            ((init_hbm, init_ref), (mg_hbm, mg_ref), (lg_hbm, lg_ref), (beta_hbm, beta_ref))
        )
    ]
    for copy in small:
        copy.start()
    for n in range(NSEG):
        kv_term(n)
    tot_ref[...] = (kv_ref[0] + kv_ref[1]) + (kv_ref[2] + kv_ref[3])
    mate_send().start()
    mate_send().wait_recv()
    chip_ref[...] = tot_ref[...] + trecv[0]
    for d in range(1, NX):

        @pl.when(z + d < NX)
        def _(d=d):
            prefix_send(d).start()

    for p in range(3):
        forward_own(p)
    for n in range(NSEG):
        load(2, n).wait()
    for copy in small:
        copy.wait()
    for i in range(8):
        own(i).wait()

    gate = 1.0 / (1.0 + jnp.exp(-jnp.full((1, HD), beta_ref[0], F32)))
    mem_scale = gate * mg_ref[...]
    loc_scale = (1.0 - gate) * lg_ref[...]

    def offsets(k):
        return pick(k, [o[0] for o in ORDER]), pick(k, [o[1] for o in ORDER])

    def send_block(k):
        dy, dx = offsets(k)
        return remote(ho.at[k], recv.at[k], h_s.at[k], h_r.at[k], head_dev(dy, dx))

    def step(k, carry):
        dy, dx = offsets(k)
        n, b = at(y, dy), at(x, dx)
        base = pl.multiple_of(n * SEG, SEG)
        for bb in range(4):

            @pl.when(b == bb)
            def _(bb=bb):
                attend(bb, base, q_ref, k_ref, v_ref, s_ref, acc_ref)

        @pl.when(k == 0)
        def _():
            forward_own(3)
            base_ref[...] = init_ref[0]
            for d in range(1, NX):

                @pl.when(z - d >= 0)
                def _(d=d):
                    prefix_send(d).wait_recv()
                    base_ref[...] += trecv[d]

            @pl.when(c == 1)
            def _():
                base_ref[...] += trecv[0]

            running = base_ref[...]
            prefix_ref[0, 0] = running * (NSEG * SEG) ** -0.5
            for m in range(NSEG):
                top = running.astype(BF16)
                memcat[m, 0:HD, :] = top
                memcat[m, HD : 2 * HD, :] = (running - top.astype(F32)).astype(BF16)
                if m < NSEG - 1:
                    running = running + kv_ref[m]

        feat = feature(q_ref[pl.ds(pl.multiple_of(base + b * BLK, BLK), BLK), :])
        read = jnp.dot(
            jnp.concatenate([feat, feat], axis=1), memcat[n], preferred_element_type=F32
        )
        read_sq = jnp.mean(read * read, axis=-1, keepdims=True)
        total = acc_ref[:, 0:HD]
        weight = acc_ref[:, HD : HD + 1]
        total_sq = jnp.mean(total * total, axis=-1, keepdims=True)
        mixed = (read * lax.rsqrt(read_sq + EPS)) * mem_scale + (
            total * lax.rsqrt(total_sq + EPS * (weight * weight))
        ) * loc_scale
        mixed = mixed.astype(BF16)

        @pl.when(k < 15)
        def _():
            ho[k] = mixed

        @pl.when(k == 15)
        def _():
            recv[15] = mixed

        for when, todo in SERVICE.items():

            @pl.when(k == when)
            def _(todo=todo):
                for what, p in todo:
                    (forward_own if what == "own" else forward_z)(p)

        @pl.when(k == HOLD)
        def _():
            def send(i, carry):
                send_block(i).start()
                return carry

            lax.fori_loop(0, HOLD, send, 0)

        @pl.when((k >= HOLD) & (k < 15))
        def _():
            send_block(k).start()

        return carry

    lax.fori_loop(0, 16, step, 0)

    def slice_at(j):
        dz = pick(j // 2, [0, 3, 1, 2])
        return at(z, dz) * 2 + lax.rem(c + j, 2)

    def arrived(slots):
        for i in slots:
            send_block(i).wait_recv()

    def project(slots, js, first):
        act = jnp.concatenate([recv[i] for i in slots], axis=1)
        for j in js:
            sl = slice_at(j)
            cols = pl.ds(pl.multiple_of(sl * WS, WS), WS)
            wt = [w8[sl, at(y, NX - ORDER[i][0]), at(x, NX - ORDER[i][1])] for i in slots]
            r = jnp.dot(act, jnp.concatenate(wt, axis=0), preferred_element_type=F32)
            if not first:
                r = oacc[:, cols] + r
            oacc[:, cols] = r

    near, far = range(6), range(6, 8)
    done = [i for i in range(16) if i not in LAST]
    early = [i for i in done if ORDER[i][0] in (0, 1)]
    late = [i for i in done if i not in early]
    for p in range(6):
        stage_c(0, p).wait_recv()
    arrived(range(0, 4))
    project(range(0, 4), (0, 1, 2, 4), True)
    for p in (0, 1, 2, 3):
        forward_r(p)
    arrived(range(4, 8))
    project(range(4, 8), (0, 1, 2, 4), False)
    for dz in (3, 1):
        for p in range(6):
            stage_c(dz, p).wait_recv()
    project(range(0, 8), (3, 5), True)
    for p in (4, 5):
        forward_r(p)
    arrived(range(12, 15))
    project(range(12, 16), near, False)
    for p in (0, 1, 2, 3):
        stage_c(2, p).wait_recv()
    project(early, far, True)
    for p in (4, 5):
        stage_c(2, p).wait_recv()
    project(late, far, False)
    arrived(LAST)

    for dy in range(NX):
        for dx in range(NX):
            if dy or dx:
                stage_a(dy, dx).wait_send()
    for p in range(6):
        stage_z(p, 0).wait_send()
        stage_z(p, 1).wait_send()
        for dz in range(4):
            stage_c(dz, p).wait_send()
    for i in range(4):
        stage_e(i).wait_send()
    for i in range(len(RELAY)):
        stage_r(i).wait_send()
    mate_send().wait_send()
    for d in range(1, NX):

        @pl.when(z + d < NX)
        def _(d=d):
            prefix_send(d).wait_send()

    def sent(k, carry):
        send_block(k).wait_send()
        return carry

    lax.fori_loop(0, 15, sent, 0)


def finish(acc_ref, recv_ref, w_ref, p_ref, a_out, p_out, o_ref, sem):
    copies = [pltpu.make_async_copy(p_ref, p_out, sem.at[8])]
    copies[0].start()
    h = lax.axis_index("head")
    y, x = h // NX, lax.rem(h, NX)
    act = jnp.concatenate([recv_ref[i] for i in LAST], axis=1)
    for sl in range(8):
        cols = pl.ds(sl * WS, WS)
        wt = [
            w_ref[sl, lax.rem(y + NX - ORDER[i][0], NX), lax.rem(x + NX - ORDER[i][1], NX)]
            for i in LAST
        ]
        r = jnp.dot(act, jnp.concatenate(wt, axis=0), preferred_element_type=F32)
        o_ref[:, cols] = (acc_ref[:, cols] + r).astype(BF16)
        copies.append(pltpu.make_async_copy(o_ref.at[:, cols], a_out.at[:, cols], sem.at[sl]))
        copies[-1].start()
    for copy in copies:
        copy.wait()


def per_device(query, keys, values, mem_init, beta, mem_gain, loc_gain, w_out):
    tokens = query.shape[0]
    hbm = pl.BlockSpec(memory_space=pltpu.HBM)
    vmem = pl.BlockSpec(memory_space=pltpu.VMEM)
    dma = pltpu.SemaphoreType.DMA
    kept = pl.pallas_call(
        kernel,
        out_shape=(
            pltpu.VMEM((BLK, D), F32),
            pltpu.VMEM((16, BLK, HD), BF16),
            pltpu.VMEM((8, NX, NX, HD, WS), BF16),
            pltpu.VMEM((1, 1, HD, HD), F32),
        ),
        in_specs=[
            hbm, hbm, hbm, hbm, hbm, hbm, hbm, hbm,
        ],
        out_specs=(vmem,) * 4,
        scratch_shapes=[
            pltpu.VMEM((tokens, HD), BF16),
            pltpu.VMEM((tokens, HD), BF16),
            pltpu.VMEM((tokens, HD), BF16),
            pltpu.VMEM((NSEG, HD, HD), F32),
            pltpu.VMEM((HD, HD), F32),
            pltpu.VMEM((HD, HD), F32),
            pltpu.VMEM((NX, HD, HD), F32),
            pltpu.VMEM((HD, HD), F32),
            pltpu.VMEM((NSEG, 2 * HD, HD), BF16),
            pltpu.VMEM((BLK, SEG), F32),
            pltpu.VMEM((BLK, 2 * HD), F32),
            pltpu.VMEM((15, BLK, HD), BF16),
            pltpu.SMEM((1,), F32),
            pltpu.VMEM((1, HD, HD), F32),
            pltpu.VMEM((1, HD), F32),
            pltpu.VMEM((1, HD), F32),
            dma((12,)), dma((8,)), dma((4,)),
            dma((16,)), dma((16,)), dma((12,)), dma((12,)), dma((11,)), dma((11,)),
            dma((4,)), dma((4,)),
            dma((24,)), dma((24,)), dma((4,)), dma((4,)), dma((15,)), dma((15,)),
        ],
        compiler_params=pltpu.CompilerParams(
            collective_id=0, has_side_effects=True, vmem_limit_bytes=40 * 2**20
        ),
        name="layer",
    )(
        beta, query, keys, values, mem_init,
        mem_gain.reshape(1, HD), loc_gain.reshape(1, HD), w_out,
    )
    return pl.pallas_call(
        finish,
        out_shape=(
            jax.ShapeDtypeStruct((BLK, D), BF16),
            jax.ShapeDtypeStruct((1, 1, HD, HD), F32),
        ),
        in_specs=[vmem] * 4,
        out_specs=(hbm, hbm),
        scratch_shapes=[pltpu.VMEM((BLK, D), BF16), dma((9,))],
        compiler_params=pltpu.CompilerParams(vmem_limit_bytes=16 * 2**20),
        name="finish",
    )(*[pltpu.with_memory_space_constraint(part, pltpu.VMEM) for part in kept])


def solution(mesh):
    in_specs = (
        P("seq", "head"),
        P("seq", "head"),
        P("seq", "head"),
        P("head", None, None),
        P("head"),
        P("head"),
        P("head"),
        P("head", None),
    )
    out_specs = (P(("seq", "head"), None), P("seq", "head", None, None))
    return jax.shard_map(
        per_device, mesh=mesh, in_specs=in_specs, out_specs=out_specs, check_vma=False
    )
```

```python
import functools
import math

import jax
import jax.numpy as jnp
from jax import lax
from jax.experimental import pallas as pl
from jax.experimental.pallas import tpu as pltpu
from jax.sharding import PartitionSpec as P

HD = 128
SEG = 2048
BLK = 512
D = 2048
NSEG = 4
NX = 4
WS = 256
EPS = 1e-06
MESH = pl.DeviceIdType.MESH
F32 = jnp.float32
BF16 = jnp.bfloat16
C2 = HD**-0.5 * math.log2(math.e)


def attend(b, base, q_ref, k_ref, v_ref, s_ref, acc_ref):
    half = BLK // 2
    q = q_ref[pl.ds(pl.multiple_of(base + b * BLK, BLK), BLK), :]

    def score(row0, rows, key0, cols, masked):
        k = k_ref[pl.ds(pl.multiple_of(base + key0, 256), cols), :]
        s = lax.dot_general(
            q[row0 : row0 + rows], k, (((1,), (1,)), ((), ())), preferred_element_type=F32
        )
        s = s * C2
        if masked:
            col = lax.broadcasted_iota(jnp.int32, (rows, cols), 1) + (key0 - b * BLK)
            row = lax.broadcasted_iota(jnp.int32, (rows, cols), 0) + row0
            s = jnp.where(col <= row, s, -jnp.inf)
        s_ref[row0 : row0 + rows, key0 : key0 + cols] = s
        top = s[:, 0:128]
        for t in range(1, cols // 128):
            top = jnp.maximum(top, s[:, t * 128 : (t + 1) * 128])
        return top

    tops = [None, None]

    def merge(i, top):
        tops[i] = top if tops[i] is None else jnp.maximum(tops[i], top)

    for key0 in range(0, b * BLK, BLK):
        top = score(0, BLK, key0, BLK, False)
        merge(0, top[:half])
        merge(1, top[half:])
    merge(1, score(half, half, b * BLK, half, False))
    merge(0, score(0, half, b * BLK, half, True))
    merge(1, score(half, half, b * BLK + half, half, True))
    for i in range(2):
        largest = jnp.max(tops[i], axis=1, keepdims=True)
        length = b * BLK + (i + 1) * half
        rows = slice(i * half, (i + 1) * half)
        p = jnp.exp2(s_ref[rows, 0:length] - largest).astype(BF16)
        v = v_ref[pl.ds(pl.multiple_of(base, SEG), length), :]
        v = jnp.concatenate([v, jnp.ones((length, HD), BF16)], axis=1)
        acc_ref[rows, :] = jnp.dot(p, v, preferred_element_type=F32)


def feature(x):
    x = x.astype(F32)
    return jnp.where(x > 0, x + 1.0, jnp.exp(x)).astype(BF16)


ORDER = (
    (2, 2), (1, 1), (3, 3), (3, 1), (1, 3), (1, 2), (2, 1), (3, 2),
    (2, 3), (1, 0), (3, 0), (2, 0), (0, 1), (0, 3), (0, 2), (0, 0),
)
HOLD = 2
LAST = (8, 9, 10, 11)
NEAR = ((0, 1), (0, 3), (1, 0), (3, 0))
NEAR_PIECE = (0, 1, 3, 4)
RELAY = (
    (2, 0, 2, True),
    (3, 1, 1, False), (3, 1, 3, False), (3, 1, 2, False),
    (4, 3, 1, True), (4, 3, 3, True), (4, 3, 2, True),
    (5, 2, 0, True), (5, 2, 1, True), (5, 2, 2, False), (5, 2, 3, False),
)
SERVICE = {
    1: (("own", 4),),
    3: (("own", 5), ("z", 0), ("z", 1), ("z", 2)),
    6: (("z", 3),),
    10: (("z", 4),),
    13: (("z", 5),),
}


def pick(k, table):
    if isinstance(k, int):
        return table[k]
    value = jnp.int32(table[0])
    for i in range(1, len(table)):
        value = jnp.where(k == i, jnp.int32(table[i]), value)
    return value


def kernel(
    beta_hbm, q_hbm, k_hbm, v_hbm, init_hbm, mg_hbm, lg_hbm, w_hbm,
    oacc, recv, w8, prefix_ref,
    q_ref, k_ref, v_ref, kv_ref, tot_ref, chip_ref, trecv, base_ref, memcat, s_ref, acc_ref,
    ho, beta_ref, init_ref, mg_ref, lg_ref, lsem, wsem, psem,
    a_s, a_r, z_s, z_r, r_s, r_r, e_s, e_r, c_s, c_r, t_s, t_r, h_s, h_r,
):
    s = lax.axis_index("seq")
    h = lax.axis_index("head")
    z, c = s // 2, lax.rem(s, 2)
    y, x = h // NX, lax.rem(h, NX)

    def at(v, d):
        return lax.rem(v + d, NX)

    def head_dev(dy, dx):
        return (s, at(y, dy) * NX + at(x, dx))

    def z_dev(d):
        return (at(z, d) * 2 + c, h)

    mate = (z * 2 + (1 - c), h)

    def remote(src, dst, ssem, rsem, dev):
        return pltpu.make_async_remote_copy(
            src_ref=src, dst_ref=dst, send_sem=ssem, recv_sem=rsem,
            device_id=dev, device_id_type=MESH,
        )

    barrier = pltpu.get_barrier_semaphore()

    def greet_head(i, carry):
        pl.semaphore_signal(
            barrier, inc=1, device_id=(s, lax.rem(h + i, 16)), device_id_type=MESH
        )
        return carry

    lax.fori_loop(1, 16, greet_head, 0)

    for dev in (mate, z_dev(1), z_dev(2), z_dev(3)):
        pl.semaphore_signal(barrier, inc=1, device_id=dev, device_id_type=MESH)

    def load(which, n):
        src = (k_hbm, v_hbm, q_hbm)[which]
        dst = (k_ref, v_ref, q_ref)[which]
        span = pl.ds(n * SEG, SEG)
        return pltpu.make_async_copy(src.at[span], dst.at[span], lsem.at[which * NSEG + n])

    def slice_of(dz):
        return at(z, dz) * 2 + c

    def own(i):
        sl = lax.rem(slice_of(0) + i, 8)
        return pltpu.make_async_copy(
            w_hbm.at[:, pl.ds(pl.multiple_of(sl * WS, WS), WS)], w8.at[sl, y, x], wsem.at[i]
        )

    for n in range(NSEG):
        load(0, n).start()
        load(1, n).start()

    def stage_a(dy, dx):
        i = dy * NX + dx
        src = w_hbm.at[:, pl.ds(pl.multiple_of(slice_of(0) * WS, WS), WS)]
        return remote(
            src, w8.at[slice_of(0), y, x], a_s.at[i], a_r.at[i], head_dev(dy, dx)
        )

    PIECES = ((0, 1), (0, 3), (0, 2), (1, None), (3, None), (2, None))

    def piece(dz, p):
        dy, dx = PIECES[p]
        if dx is None:
            return w8.at[slice_of(dz), at(y, NX - dy)]
        return w8.at[slice_of(dz), y, at(x, NX - dx)]

    def stage_z(p, way):
        ref = piece(0, p)
        return remote(
            ref, ref, z_s.at[p * 2 + way], z_r.at[p * 2 + way], z_dev(1 if way == 0 else 3)
        )

    def stage_e(i):
        dy, dx = NEAR[i]
        sl = slice_of(2)
        src = w_hbm.at[:, pl.ds(pl.multiple_of(sl * WS, WS), WS)]
        return remote(src, w8.at[sl, y, x], e_s.at[i], e_r.at[i], head_dev(dy, dx))

    def stage_r(i):
        _, dy, dx, up = RELAY[i]
        ref = w8.at[slice_of(3 if up else 1), at(y, NX - dy), at(x, NX - dx)]
        return remote(ref, ref, r_s.at[i], r_r.at[i], z_dev(1 if up else 3))

    def stage_c(dz, p):
        ref = piece(dz, p)
        return remote(ref, ref, c_s.at[dz * 6 + p], c_r.at[dz * 6 + p], mate)

    def forward_own(p):
        dy, dx = PIECES[p]
        for d in range(NX) if dx is None else (dx,):
            stage_a(dy, d).wait_recv()
        stage_z(p, 0).start()
        stage_z(p, 1).start()
        stage_c(0, p).start()

    def forward_z(p):
        for way in range(2):
            stage_z(p, way).wait_recv()
            for i, (piece_of, _, _, up) in enumerate(RELAY):
                if piece_of == p and up == (way == 0):
                    stage_r(i).start()
            stage_c(3 if way == 0 else 1, p).start()

    def forward_r(p):
        if p in NEAR_PIECE:
            stage_e(NEAR_PIECE.index(p)).wait_recv()
        for i, relay in enumerate(RELAY):
            if relay[0] == p:
                stage_r(i).wait_recv()
        stage_c(2, p).start()

    def mate_send():
        return remote(tot_ref, trecv.at[0], t_s.at[0], t_r.at[0], mate)

    def prefix_send(d):
        return remote(chip_ref, trecv.at[d], t_s.at[d], t_r.at[d], z_dev(d))

    def kv_term(n):
        load(0, n).wait()
        load(1, n).wait()
        span = slice(n * SEG, (n + 1) * SEG)
        kv_ref[n] = lax.dot_general(
            feature(k_ref[span, :]), v_ref[span, :], (((0,), (0,)), ((), ())),
            preferred_element_type=F32,
        )

    pl.semaphore_wait(barrier, 19)
    for dy in (0, 1, 3, 2):
        for dx in (1, 3, 0, 2):
            if dy or dx:
                stage_a(dy, dx).start()
    for i in range(4):
        stage_e(i).start()
    for n in range(NSEG):
        load(2, n).start()
    for i in range(8):
        own(i).start()
    small = [
        pltpu.make_async_copy(src, dst, psem.at[i])
        for i, (src, dst) in enumerate(
            ((init_hbm, init_ref), (mg_hbm, mg_ref), (lg_hbm, lg_ref), (beta_hbm, beta_ref))
        )
    ]
    for copy in small:
        copy.start()
    for n in range(NSEG):
        kv_term(n)
    tot_ref[...] = (kv_ref[0] + kv_ref[1]) + (kv_ref[2] + kv_ref[3])
    mate_send().start()
    mate_send().wait_recv()
    chip_ref[...] = tot_ref[...] + trecv[0]
    for d in range(1, NX):

        @pl.when(z + d < NX)
        def _(d=d):
            prefix_send(d).start()

    for p in range(3):
        forward_own(p)
    for n in range(NSEG):
        load(2, n).wait()
    for copy in small:
        copy.wait()
    for i in range(8):
        own(i).wait()

    gate = 1.0 / (1.0 + jnp.exp(-jnp.full((1, HD), beta_ref[0], F32)))
    mem_scale = gate * mg_ref[...]
    loc_scale = (1.0 - gate) * lg_ref[...]

    def offsets(k):
        return pick(k, [o[0] for o in ORDER]), pick(k, [o[1] for o in ORDER])

    def send_block(k):
        dy, dx = offsets(k)
        return remote(ho.at[k], recv.at[k], h_s.at[k], h_r.at[k], head_dev(dy, dx))

    def step(k, carry):
        dy, dx = offsets(k)
        n, b = at(y, dy), at(x, dx)
        base = pl.multiple_of(n * SEG, SEG)
        for bb in range(4):

            @pl.when(b == bb)
            def _(bb=bb):
                attend(bb, base, q_ref, k_ref, v_ref, s_ref, acc_ref)

        @pl.when(k == 0)
        def _():
            forward_own(3)
            base_ref[...] = init_ref[0]
            for d in range(1, NX):

                @pl.when(z - d >= 0)
                def _(d=d):
                    prefix_send(d).wait_recv()
                    base_ref[...] += trecv[d]

            @pl.when(c == 1)
            def _():
                base_ref[...] += trecv[0]

            running = base_ref[...]
            prefix_ref[0, 0] = running * (NSEG * SEG) ** -0.5
            for m in range(NSEG):
                top = running.astype(BF16)
                memcat[m, 0:HD, :] = top
                memcat[m, HD : 2 * HD, :] = (running - top.astype(F32)).astype(BF16)
                if m < NSEG - 1:
                    running = running + kv_ref[m]

        feat = feature(q_ref[pl.ds(pl.multiple_of(base + b * BLK, BLK), BLK), :])
        read = jnp.dot(
            jnp.concatenate([feat, feat], axis=1), memcat[n], preferred_element_type=F32
        )
        read_sq = jnp.mean(read * read, axis=-1, keepdims=True)
        total = acc_ref[:, 0:HD]
        weight = acc_ref[:, HD : HD + 1]
        total_sq = jnp.mean(total * total, axis=-1, keepdims=True)
        mixed = (read * lax.rsqrt(read_sq + EPS)) * mem_scale + (
            total * lax.rsqrt(total_sq + EPS * (weight * weight))
        ) * loc_scale
        mixed = mixed.astype(BF16)

        @pl.when(k < 15)
        def _():
            ho[k] = mixed

        @pl.when(k == 15)
        def _():
            recv[15] = mixed

        for when, todo in SERVICE.items():

            @pl.when(k == when)
            def _(todo=todo):
                for what, p in todo:
                    (forward_own if what == "own" else forward_z)(p)

        @pl.when(k == HOLD)
        def _():
            def send(i, carry):
                send_block(i).start()
                return carry

            lax.fori_loop(0, HOLD, send, 0)

        @pl.when((k >= HOLD) & (k < 15))
        def _():
            send_block(k).start()

        return carry

    lax.fori_loop(0, 16, step, 0)

    def slice_at(j):
        dz = pick(j // 2, [0, 3, 1, 2])
        return at(z, dz) * 2 + lax.rem(c + j, 2)

    def arrived(slots):
        for i in slots:
            send_block(i).wait_recv()

    def project(slots, js, first):
        act = jnp.concatenate([recv[i] for i in slots], axis=1)
        for j in js:
            sl = slice_at(j)
            cols = pl.ds(pl.multiple_of(sl * WS, WS), WS)
            wt = [w8[sl, at(y, NX - ORDER[i][0]), at(x, NX - ORDER[i][1])] for i in slots]
            r = jnp.dot(act, jnp.concatenate(wt, axis=0), preferred_element_type=F32)
            if not first:
                r = oacc[:, cols] + r
            oacc[:, cols] = r

    near, far = range(6), range(6, 8)
    done = [i for i in range(16) if i not in LAST]
    early = [i for i in done if ORDER[i][0] in (0, 1)]
    late = [i for i in done if i not in early]
    for p in range(6):
        stage_c(0, p).wait_recv()
    arrived(range(0, 4))
    project(range(0, 4), (0, 1, 2, 4), True)
    for p in (0, 1, 2, 3):
        forward_r(p)
    arrived(range(4, 8))
    project(range(4, 8), (0, 1, 2, 4), False)
    for dz in (3, 1):
        for p in range(6):
            stage_c(dz, p).wait_recv()
    project(range(0, 8), (3, 5), True)
    for p in (4, 5):
        forward_r(p)
    arrived(range(12, 15))
    project(range(12, 16), near, False)
    for p in (0, 1, 2, 3):
        stage_c(2, p).wait_recv()
    project(early, far, True)
    for p in (4, 5):
        stage_c(2, p).wait_recv()
    project(late, far, False)
    arrived(LAST)

    for dy in range(NX):
        for dx in range(NX):
            if dy or dx:
                stage_a(dy, dx).wait_send()
    for p in range(6):
        stage_z(p, 0).wait_send()
        stage_z(p, 1).wait_send()
        for dz in range(4):
            stage_c(dz, p).wait_send()
    for i in range(4):
        stage_e(i).wait_send()
    for i in range(len(RELAY)):
        stage_r(i).wait_send()
    mate_send().wait_send()
    for d in range(1, NX):

        @pl.when(z + d < NX)
        def _(d=d):
            prefix_send(d).wait_send()

    def sent(k, carry):
        send_block(k).wait_send()
        return carry

    lax.fori_loop(0, 15, sent, 0)


def finish(acc_ref, recv_ref, w_ref, p_ref, a_out, p_out, o_ref, sem):
    copies = [pltpu.make_async_copy(p_ref, p_out, sem.at[8])]
    copies[0].start()
    h = lax.axis_index("head")
    y, x = h // NX, lax.rem(h, NX)
    act = jnp.concatenate([recv_ref[i] for i in LAST], axis=1)
    for sl in range(8):
        cols = pl.ds(sl * WS, WS)
        wt = [
            w_ref[sl, lax.rem(y + NX - ORDER[i][0], NX), lax.rem(x + NX - ORDER[i][1], NX)]
            for i in LAST
        ]
        r = jnp.dot(act, jnp.concatenate(wt, axis=0), preferred_element_type=F32)
        o_ref[:, cols] = (acc_ref[:, cols] + r).astype(BF16)
        copies.append(pltpu.make_async_copy(o_ref.at[:, cols], a_out.at[:, cols], sem.at[sl]))
        copies[-1].start()
    for copy in copies:
        copy.wait()


def per_device(query, keys, values, mem_init, beta, mem_gain, loc_gain, w_out):
    tokens = query.shape[0]
    hbm = pl.BlockSpec(memory_space=pltpu.HBM)
    vmem = pl.BlockSpec(memory_space=pltpu.VMEM)
    dma = pltpu.SemaphoreType.DMA
    kept = pl.pallas_call(
        kernel,
        out_shape=(
            pltpu.VMEM((BLK, D), F32),
            pltpu.VMEM((16, BLK, HD), BF16),
            pltpu.VMEM((8, NX, NX, HD, WS), BF16),
            pltpu.VMEM((1, 1, HD, HD), F32),
        ),
        in_specs=[
            hbm, hbm, hbm, hbm, hbm, hbm, hbm, hbm,
        ],
        out_specs=(vmem,) * 4,
        scratch_shapes=[
            pltpu.VMEM((tokens, HD), BF16),
            pltpu.VMEM((tokens, HD), BF16),
            pltpu.VMEM((tokens, HD), BF16),
            pltpu.VMEM((NSEG, HD, HD), F32),
            pltpu.VMEM((HD, HD), F32),
            pltpu.VMEM((HD, HD), F32),
            pltpu.VMEM((NX, HD, HD), F32),
            pltpu.VMEM((HD, HD), F32),
            pltpu.VMEM((NSEG, 2 * HD, HD), BF16),
            pltpu.VMEM((BLK, SEG), F32),
            pltpu.VMEM((BLK, 2 * HD), F32),
            pltpu.VMEM((15, BLK, HD), BF16),
            pltpu.SMEM((1,), F32),
            pltpu.VMEM((1, HD, HD), F32),
            pltpu.VMEM((1, HD), F32),
            pltpu.VMEM((1, HD), F32),
            dma((12,)), dma((8,)), dma((4,)),
            dma((16,)), dma((16,)), dma((12,)), dma((12,)), dma((11,)), dma((11,)),
            dma((4,)), dma((4,)),
            dma((24,)), dma((24,)), dma((4,)), dma((4,)), dma((15,)), dma((15,)),
        ],
        compiler_params=pltpu.CompilerParams(
            collective_id=0, has_side_effects=True, vmem_limit_bytes=40 * 2**20
        ),
        name="layer",
    )(
        beta, query, keys, values, mem_init,
        mem_gain.reshape(1, HD), loc_gain.reshape(1, HD), w_out,
    )
    return pl.pallas_call(
        finish,
        out_shape=(
            jax.ShapeDtypeStruct((BLK, D), BF16),
            jax.ShapeDtypeStruct((1, 1, HD, HD), F32),
        ),
        in_specs=[vmem] * 4,
        out_specs=(hbm, hbm),
        scratch_shapes=[pltpu.VMEM((BLK, D), BF16), dma((9,))],
        compiler_params=pltpu.CompilerParams(vmem_limit_bytes=16 * 2**20),
        name="finish",
    )(*[pltpu.with_memory_space_constraint(part, pltpu.VMEM) for part in kept])


def solution(mesh):
    in_specs = (
        P("seq", "head"),
        P("seq", "head"),
        P("seq", "head"),
        P("head", None, None),
        P("head"),
        P("head"),
        P("head"),
        P("head", None),
    )
    out_specs = (P(("seq", "head"), None), P("seq", "head", None, None))
    return jax.shard_map(
        per_device, mesh=mesh, in_specs=in_specs, out_specs=out_specs, check_vma=False
    )
```
